32 devices in a mesh: group: 2 (over y), shard: 16 (over z, x, core).
Axes of the slice: x: 2, y: 2, z: 4, core: 2. Of those that a mesh axis runs over, the one named last changes fastest.
Arguments:
- samples: bfloat16 [32, 8192], P('shard'), may hold values from -6 to 6
- factor_old: float32 [8192, 8192], P('shard', 'group'), as said below
- damping: float32 [1], replicated, may hold values from 0.1 to 1
- gradients: bfloat16 [2048, 8192], P('shard', 'group'), may hold values from -6 to 6
Outputs:
- swept_factor: float32 [8192, 8192], P('shard', 'group')
- update: bfloat16 [8192, 2048], P('shard', 'group')
The draws below stay inside these ranges and needn't reach their ends.
Inputs may be any that keep to these rules, and one draw needn't show every extreme that they name: factor_old is symmetric and positive definite.
All inputs are finite; a program needn't handle non-finite values.
Results may differ from the reference program's by a relative error of at most 0.0049.
Values may be sent and summed in bfloat16 or wider, within the bound.
A program may use at most 128 MiB of HBM per device.

```python
import math
import jax
import jax.numpy as jnp
from jax import lax

D = 8192
KV = 1024
BLOCK = 128
PIVOTS = 2
TOKENS_S = 32


def draw_factor_old(key, part):
    key_diag, key_hist = jax.random.split(key)
    diag_scale = jnp.exp(jax.random.uniform(key_diag, (D,), jnp.float32, math.log(0.5), math.log(2.0)))
    history = D // 16
    signs = (jax.random.randint(key_hist, (history, D), 0, 2) * 2 - 1).astype(jnp.float32)
    gram = lax.dot_general(signs, signs, (((0,), (0,)), ((), ())), precision=lax.Precision.HIGHEST, preferred_element_type=jnp.float32)
    identity = jnp.eye(D, dtype=jnp.float32)
    running = gram / history + 0.5 * identity
    root_scale = jnp.sqrt(diag_scale)
    return root_scale[:, None] * running * root_scale[None, :]


def shard_levels(key, dims, cuts, low, top_value):
    loudness, own = 1.0, jax.random.fold_in(key, 6)
    for dim, parts in cuts:
        steps = jnp.exp(jax.random.uniform(jax.random.fold_in(own, dim), (parts,), jnp.float32, low / len(cuts), top_value / len(cuts)))
        loudness = loudness * jnp.repeat(steps, dims[dim] // parts).reshape([-1 if axis == dim else 1 for axis in range(len(dims))])
    return loudness


def centred(key, dims, scale, limit, cuts=(), kind=jnp.bfloat16):
    array = scale * jax.random.normal(key, dims, jnp.float32)
    if cuts:
        array = array * shard_levels(key, dims, cuts, -0.22, 0.18)
    return jnp.clip(array, -limit, limit).astype(kind)


def setup_inputs(seed: int = 0) -> dict:
    key_list = jax.random.split(jax.random.key(seed), 5)
    return {
        "samples": centred(key_list[0], (TOKENS_S, D), 1.0, 6.0, ((0, 16),)),
        "factor_old": draw_factor_old(jax.random.fold_in(key_list[4], 71), 0),
        "damping": jnp.clip(jnp.exp(jax.random.uniform(key_list[2], (1,), jnp.float32, math.log(0.1), math.log(1.0))), 0.1, 1.0),
        "gradients": centred(key_list[3], (2 * KV, D), 1.0, 6.0, ((0, 16), (1, 2))),
    }


ema_keep = 0.5

def solve_spd(pivot_block, right_side):
    lower_factor = jnp.linalg.cholesky(pivot_block)
    half_solved = lax.linalg.triangular_solve(lower_factor, right_side, left_side=True, lower=True)
    return lax.linalg.triangular_solve(lower_factor, half_solved, left_side=True, lower=True, transpose_a=True)

def reference(samples, factor_old, damping, gradients):
    covariance = jnp.dot(samples.T.astype(jnp.float32), samples.astype(jnp.float32), preferred_element_type=jnp.float32) / TOKENS_S
    identity = jnp.eye(D, dtype=jnp.float32)
    factor = ema_keep * factor_old + (1.0 - ema_keep) * covariance + damping[0] * identity
    spacing = D // PIVOTS
    sel_rows = lax.broadcasted_iota(jnp.int32, (BLOCK, D), 0)
    sel_cols = lax.broadcasted_iota(jnp.int32, (BLOCK, D), 1)

    def sweep_once(sweep_step, matrix):
        first_index = (sweep_step * spacing).astype(jnp.int32)
        pivot_strip = lax.dynamic_slice_in_dim(matrix, first_index, BLOCK, 0)
        column = lax.dynamic_slice_in_dim(matrix, first_index, BLOCK, 1)
        pivot_block = lax.dynamic_slice_in_dim(pivot_strip, first_index, BLOCK, 1)
        selector = jnp.where(sel_cols == sel_rows + first_index, 1.0, 0.0).astype(jnp.float32)
        factor_q = solve_spd(pivot_block, pivot_strip + selector)
        matrix = matrix - jnp.dot(column.astype(jnp.float32), factor_q.astype(jnp.float32), precision=lax.Precision.HIGHEST, preferred_element_type=jnp.float32)
        block_rows = lax.dynamic_slice_in_dim(matrix, first_index, BLOCK, 0) + factor_q
        return lax.dynamic_update_slice_in_dim(matrix, block_rows, first_index, 0)
    swept_factor = lax.fori_loop(0, PIVOTS, sweep_once, factor)
    swept_half = swept_factor.astype(jnp.bfloat16)
    update = lax.dot_general(swept_half.astype(jnp.float32), gradients.astype(jnp.float32), (((1,), (1,)), ((), ())), preferred_element_type=jnp.float32)
    return (swept_factor, update.astype(jnp.bfloat16))
```

```python
import jax
import jax.numpy as jnp
from jax import lax
from jax.sharding import PartitionSpec as P

D = 8192
BLOCK = 128
PIVOTS = 2


ema_keep = 0.5


def spread(block, axis, holder):
    block = jnp.where(lax.axis_index(axis) == holder, block, jnp.zeros_like(block))
    return lax.psum(block, axis)


def solve_spd(pivot_block, right_side):
    lower_factor = jnp.linalg.cholesky(pivot_block)
    half_solved = lax.linalg.triangular_solve(lower_factor, right_side, left_side=True, lower=True)
    return lax.linalg.triangular_solve(
        lower_factor, half_solved, left_side=True, lower=True, transpose_a=True
    )


def on_device(samples, factor_old, damping, gradients):
    row_count, col_count = factor_old.shape
    shard_index = lax.axis_index("shard")
    group_index = lax.axis_index("group")
    row_first = shard_index * row_count
    col_first = group_index * col_count
    total_tokens = samples.shape[0] * lax.axis_size("shard")
    contract = (((0,), (0,)), ((), ()))
    token_piece = lax.all_gather(samples, "shard", axis=0, tiled=True)
    left_part = lax.dynamic_slice_in_dim(token_piece, row_first, row_count, 1)
    right_part = lax.dynamic_slice_in_dim(token_piece, col_first, col_count, 1)
    covariance = lax.dot_general(
        left_part, right_part, contract, preferred_element_type=jnp.float32
    )
    row_ids = lax.broadcasted_iota(jnp.int32, (row_count, col_count), 0) + row_first
    col_ids = lax.broadcasted_iota(jnp.int32, (row_count, col_count), 1) + col_first
    diagonal = jnp.where(row_ids == col_ids, damping[0], 0.0)
    factor = ema_keep * factor_old + (1.0 - ema_keep) * (covariance / total_tokens) + diagonal
    spacing = D // PIVOTS
    sel_rows = lax.broadcasted_iota(jnp.int32, (BLOCK, col_count), 0)
    sel_cols = lax.broadcasted_iota(jnp.int32, (BLOCK, col_count), 1) + col_first

    def sweep_once(sweep_step, matrix):
        first_index = (sweep_step * spacing).astype(jnp.int32)
        col_owner = first_index // col_count
        row_owner = first_index // row_count
        col_offset = first_index - col_owner * col_count
        row_offset = first_index - row_owner * row_count
        own_columns = lax.dynamic_slice_in_dim(matrix, col_offset, BLOCK, 1)
        column = spread(own_columns, "group", col_owner)
        own_rows = lax.dynamic_slice_in_dim(matrix, row_offset, BLOCK, 0)
        own_pivot = lax.dynamic_slice_in_dim(column, row_offset, BLOCK, 0)
        pivot_strip, pivot_block = (
            spread(own_rows, "shard", row_owner),
            spread(own_pivot, "shard", row_owner),
        )
        selector = jnp.where(sel_cols == sel_rows + first_index, 1.0, 0.0).astype(jnp.float32)
        factor_q = solve_spd(pivot_block, pivot_strip + selector)
        matrix = matrix - jnp.dot(
            column, factor_q, precision=lax.Precision.HIGHEST, preferred_element_type=jnp.float32
        )
        addition = jnp.where(shard_index == row_owner, factor_q, 0.0)
        block_rows = lax.dynamic_slice_in_dim(matrix, row_offset, BLOCK, 0) + addition
        return lax.dynamic_update_slice_in_dim(matrix, block_rows, row_offset, 0)

    swept_factor = lax.fori_loop(0, PIVOTS, sweep_once, factor)
    swept_half = swept_factor.astype(jnp.bfloat16)
    partial_terms = lax.dot_general(
        swept_half,
        lax.all_gather(gradients, "shard", axis=0, tiled=True),
        (((1,), (1,)), ((), ())),
        preferred_element_type=jnp.float32,
    )
    update = lax.psum_scatter(partial_terms, "group", scatter_dimension=1, tiled=True).astype(
        jnp.bfloat16
    )
    return (swept_factor, update)


def damped(old, left, right, total, hit, damping):
    cov = lax.dot_general(left, right, (((0,), (0,)), ((), ())), preferred_element_type=jnp.float32)
    return ema_keep * old + (1.0 - ema_keep) * (cov / total) + jnp.where(hit, damping, 0.0)


def exact(a, b):
    return jnp.dot(a, b, precision=lax.Precision.HIGHEST, preferred_element_type=jnp.float32)


def on_device_pairs(samples, factor_old, damping, gradients):
    rows, cols = factor_old.shape
    shards = lax.axis_size("shard")
    shard = lax.axis_index("shard")
    group = lax.axis_index("group")
    row_first, col_first = shard * rows, group * cols
    total = samples.shape[0] * shards
    wide = PIVOTS * BLOCK
    bf16, f32 = jnp.bfloat16, jnp.float32
    own = factor_old[:, :BLOCK]
    high = own.astype(bf16)
    low = (own[:BLOCK] - high[:BLOCK].astype(f32)).astype(bf16)
    flat = samples.reshape(-1, BLOCK)
    packed = jnp.concatenate([high, low, flat], axis=0)
    everyone = lax.all_gather(packed, ("group", "shard"), axis=0, tiled=False)
    units = gradients.shape[0] // 2
    gathered = []
    for half in range(2):
        piece = gradients[half * units:(half + 1) * units]
        gathered.append(lax.all_gather(piece, "shard", axis=0, tiled=False))
    everyone = everyone.reshape(PIVOTS, shards, packed.shape[0], BLOCK)
    tokens = everyone[0, :, rows + BLOCK:].reshape(total, D)
    columns = everyone[:, :, :rows].reshape(PIVOTS, D, BLOCK)
    lows = everyone[:, :, rows:rows + BLOCK]
    spacing = D // PIVOTS
    ptok = jnp.concatenate([tokens[:, p * spacing:p * spacing + BLOCK] for p in range(PIVOTS)], axis=1)
    pidx = jnp.concatenate([jnp.arange(BLOCK) + p * spacing for p in range(PIVOTS)])
    left = lax.dynamic_slice_in_dim(tokens, row_first, rows, 1)
    right = lax.dynamic_slice_in_dim(tokens, col_first, cols, 1)
    rid = jnp.arange(rows) + row_first
    cid = jnp.arange(cols) + col_first
    d0 = damping[0]
    col_own = lax.dynamic_slice_in_dim(columns, row_first, rows, 1)
    col_own = jnp.concatenate([col_own[p] for p in range(PIVOTS)], axis=1).astype(f32)
    C = damped(col_own, left, ptok, total, rid[:, None] == pidx[None, :], d0)
    strip = lax.dynamic_slice_in_dim(columns, col_first, cols, 1)
    strip = jnp.concatenate([strip[p].T for p in range(PIVOTS)], axis=0).astype(f32)
    R = damped(strip, ptok, right, total, pidx[:, None] == cid[None, :], d0)
    blocks = []
    for p in range(PIVOTS):
        lo = p * spacing // rows
        blocks.append(jnp.concatenate(
            [columns[q, p * spacing:p * spacing + BLOCK].astype(f32) + lows[q, lo].astype(f32)
             for q in range(PIVOTS)], axis=1))
    A = damped(jnp.concatenate(blocks, axis=0), ptok, ptok, total, pidx[:, None] == pidx[None, :], d0)
    E = jnp.where(pidx[:, None] == cid[None, :], 1.0, 0.0).astype(f32)
    ones = jnp.eye(BLOCK, dtype=f32)
    a, b = slice(0, BLOCK), slice(BLOCK, wide)
    inv1 = solve_spd(A[a, a], ones)
    q1 = exact(inv1, R[a] + E[a])
    cross = exact(inv1, A[a, b])
    A22 = A[b, b] - exact(A[b, a], cross)
    inv2 = solve_spd(A22, ones)
    q2 = exact(inv2, R[b] - exact(A[b, a], q1) + E[b])
    rows1 = shard == 0
    C2 = C[:, b] - exact(C[:, a], cross)
    add = jnp.where(rows1, cross, 0.0)
    C2 = C2.at[:BLOCK].add(add)
    Q = jnp.concatenate([q1, q2], axis=0)
    both = jnp.concatenate([C[:, a], C2], axis=1)
    factor = damped(factor_old, left, right, total, rid[:, None] == cid[None, :], d0)
    swept = factor - jnp.dot(both, Q, precision=lax.Precision.HIGH, preferred_element_type=f32)
    owner2 = spacing // rows
    extra = jnp.where(rows1, q1, jnp.where(shard == owner2, q2, 0.0))
    swept = swept.at[:BLOCK].add(extra)
    half_swept = swept.astype(bf16)
    out = []
    for g in gathered:
        mine_first = group * (shards // PIVOTS)
        other_first = (1 - group) * (shards // PIVOTS)
        def part(first):
            piece = lax.dynamic_slice_in_dim(g, first, shards // PIVOTS, 0).reshape(-1, cols)
            return lax.dot_general(half_swept, piece, (((1,), (1,)), ((), ())), preferred_element_type=f32)
        sent = lax.ppermute(part(other_first).astype(bf16), "group", [(0, 1), (1, 0)])
        out.append((part(mine_first) + sent.astype(f32)).astype(bf16).reshape(rows, shards // PIVOTS, 1, units))
    update = jnp.concatenate(out, axis=2).reshape(rows, -1)
    return (swept, update)


def solution(mesh):
    sizes = dict(mesh.shape)
    paired = sizes["group"] == PIVOTS == 2 and (D // sizes["shard"]) >= BLOCK
    return jax.shard_map(
        on_device_pairs if paired else on_device,
        mesh=mesh,
        in_specs=(P("shard", None), P("shard", "group"), P(), P("shard", "group")),
        out_specs=(P("shard", "group"), P("shard", "group")),
        check_vma=False,
    )
```

```python
import jax
import jax.numpy as jnp
from jax import lax
from jax.sharding import PartitionSpec as P

D = 8192
BLOCK = 128
PIVOTS = 2


ema_keep = 0.5


def spread(block, axis, holder):
    block = jnp.where(lax.axis_index(axis) == holder, block, jnp.zeros_like(block))
    return lax.psum(block, axis)


def solve_spd(pivot_block, right_side):
    lower_factor = jnp.linalg.cholesky(pivot_block)
    half_solved = lax.linalg.triangular_solve(lower_factor, right_side, left_side=True, lower=True)
    return lax.linalg.triangular_solve(
        lower_factor, half_solved, left_side=True, lower=True, transpose_a=True
    )


def on_device(samples, factor_old, damping, gradients):
    row_count, col_count = factor_old.shape
    shard_index = lax.axis_index("shard")
    group_index = lax.axis_index("group")
    row_first = shard_index * row_count
    col_first = group_index * col_count
    total_tokens = samples.shape[0] * lax.axis_size("shard")
    contract = (((0,), (0,)), ((), ()))
    token_piece = lax.all_gather(samples, "shard", axis=0, tiled=True)
    left_part = lax.dynamic_slice_in_dim(token_piece, row_first, row_count, 1)
    right_part = lax.dynamic_slice_in_dim(token_piece, col_first, col_count, 1)
    covariance = lax.dot_general(
        left_part, right_part, contract, preferred_element_type=jnp.float32
    )
    row_ids = lax.broadcasted_iota(jnp.int32, (row_count, col_count), 0) + row_first
    col_ids = lax.broadcasted_iota(jnp.int32, (row_count, col_count), 1) + col_first
    diagonal = jnp.where(row_ids == col_ids, damping[0], 0.0)
    factor = ema_keep * factor_old + (1.0 - ema_keep) * (covariance / total_tokens) + diagonal
    spacing = D // PIVOTS
    sel_rows = lax.broadcasted_iota(jnp.int32, (BLOCK, col_count), 0)
    sel_cols = lax.broadcasted_iota(jnp.int32, (BLOCK, col_count), 1) + col_first

    def sweep_once(sweep_step, matrix):
        first_index = (sweep_step * spacing).astype(jnp.int32)
        col_owner = first_index // col_count
        row_owner = first_index // row_count
        col_offset = first_index - col_owner * col_count
        row_offset = first_index - row_owner * row_count
        own_columns = lax.dynamic_slice_in_dim(matrix, col_offset, BLOCK, 1)
        column = spread(own_columns, "group", col_owner)
        own_rows = lax.dynamic_slice_in_dim(matrix, row_offset, BLOCK, 0)
        own_pivot = lax.dynamic_slice_in_dim(column, row_offset, BLOCK, 0)
        pivot_strip, pivot_block = (
            spread(own_rows, "shard", row_owner),
            spread(own_pivot, "shard", row_owner),
        )
        selector = jnp.where(sel_cols == sel_rows + first_index, 1.0, 0.0).astype(jnp.float32)
        factor_q = solve_spd(pivot_block, pivot_strip + selector)
        matrix = matrix - jnp.dot(
            column, factor_q, precision=lax.Precision.HIGHEST, preferred_element_type=jnp.float32
        )
        addition = jnp.where(shard_index == row_owner, factor_q, 0.0)
        block_rows = lax.dynamic_slice_in_dim(matrix, row_offset, BLOCK, 0) + addition
        return lax.dynamic_update_slice_in_dim(matrix, block_rows, row_offset, 0)

    swept_factor = lax.fori_loop(0, PIVOTS, sweep_once, factor)
    swept_half = swept_factor.astype(jnp.bfloat16)
    partial_terms = lax.dot_general(
        swept_half,
        lax.all_gather(gradients, "shard", axis=0, tiled=True),
        (((1,), (1,)), ((), ())),
        preferred_element_type=jnp.float32,
    )
    update = lax.psum_scatter(partial_terms, "group", scatter_dimension=1, tiled=True).astype(
        jnp.bfloat16
    )
    return (swept_factor, update)


def damped(old, left, right, total, hit, damping):
    cov = lax.dot_general(left, right, (((0,), (0,)), ((), ())), preferred_element_type=jnp.float32)
    return ema_keep * old + (1.0 - ema_keep) * (cov / total) + jnp.where(hit, damping, 0.0)


def exact(a, b):
    return jnp.dot(a, b, precision=lax.Precision.HIGHEST, preferred_element_type=jnp.float32)


def on_device_pairs(samples, factor_old, damping, gradients):
    rows, cols = factor_old.shape
    shards = lax.axis_size("shard")
    shard = lax.axis_index("shard")
    group = lax.axis_index("group")
    row_first, col_first = shard * rows, group * cols
    total = samples.shape[0] * shards
    wide = PIVOTS * BLOCK
    bf16, f32 = jnp.bfloat16, jnp.float32
    half_count = shards // PIVOTS
    shard_half = shard // half_count
    own = factor_old[:, :BLOCK]
    high = own.astype(bf16)
    low = (own[:BLOCK] - high[:BLOCK].astype(f32)).astype(bf16)
    swap = [(0, 1), (1, 0)]

    def ordered(first, mine, other, axis):
        return jnp.concatenate([jnp.where(first, mine, other), jnp.where(first, other, mine)], axis=axis)

    mine = jnp.concatenate([high, low], axis=0)
    pair = ordered(group == 0, mine, lax.ppermute(mine, "group", swap), 1)
    across = [(i, i ^ half_count) for i in range(shards)]
    tokens = jnp.concatenate([samples, lax.ppermute(samples, "shard", across)], axis=0).reshape(-1, wide)
    one_way = [(g * shards + i, g * shards + (i ^ half_count))
               for g in range(PIVOTS) for i in range(shards) if i // half_count == g]
    moved = lax.ppermute(pair, ("group", "shard"), one_way)
    held = jnp.concatenate([jnp.where(shard_half == group, pair, moved), tokens], axis=0)[None]
    bits = [1 << k for k in range(half_count.bit_length() - 1)]
    bits = bits[1:] + bits[:1]
    for bit in bits:
        other = lax.ppermute(held, "shard", [(i, i ^ bit) for i in range(shards)])
        held = ordered((shard & bit) == 0, held, other, 0)
    depth = held.shape[1]
    held = jnp.swapaxes(held.reshape(2, half_count // 2, depth, wide), 0, 1)
    held = held.reshape(half_count, depth, wide)
    units = gradients.shape[0] // 2
    gathered = []
    for half in range(2):
        piece = gradients[half * units:(half + 1) * units]
        gathered.append(lax.all_gather(piece, "shard", axis=0, tiled=False))
    tokens = held[:, rows + BLOCK:].reshape(total, D)
    columns = held[:, :rows].reshape(cols, wide)
    spacing = D // PIVOTS
    ptok = jnp.concatenate([tokens[:, p * spacing:p * spacing + BLOCK] for p in range(PIVOTS)], axis=1)
    pidx = jnp.concatenate([jnp.arange(BLOCK) + p * spacing for p in range(PIVOTS)])
    left = lax.dynamic_slice_in_dim(tokens, row_first, rows, 1)
    right = lax.dynamic_slice_in_dim(tokens, col_first, cols, 1)
    rid = jnp.arange(rows) + row_first
    cid = jnp.arange(cols) + col_first
    d0 = damping[0]
    col_own = pair[:rows].astype(f32)
    C = damped(col_own, left, ptok, total, rid[:, None] == pidx[None, :], d0)
    strip = columns.T.astype(f32)
    R = damped(strip, ptok, right, total, pidx[:, None] == cid[None, :], d0)
    tops = jnp.stack([held[0, :BLOCK], held[0, rows:rows + BLOCK]])
    tops = ordered(group == 0, tops, lax.ppermute(tops, "group", swap), 1).astype(f32)
    A = damped(tops[0] + tops[1], ptok, ptok, total, pidx[:, None] == pidx[None, :], d0)
    E = jnp.where(pidx[:, None] == cid[None, :], 1.0, 0.0).astype(f32)
    ones = jnp.eye(BLOCK, dtype=f32)
    a, b = slice(0, BLOCK), slice(BLOCK, wide)
    inv1 = solve_spd(A[a, a], ones)
    q1 = exact(inv1, R[a] + E[a])
    cross = exact(inv1, A[a, b])
    A22 = A[b, b] - exact(A[b, a], cross)
    inv2 = solve_spd(A22, ones)
    q2 = exact(inv2, R[b] - exact(A[b, a], q1) + E[b])
    rows1 = shard == 0
    C2 = C[:, b] - exact(C[:, a], cross)
    add = jnp.where(rows1, cross, 0.0)
    C2 = C2.at[:BLOCK].add(add)
    Q = jnp.concatenate([q1, q2], axis=0)
    both = jnp.concatenate([C[:, a], C2], axis=1)
    factor = damped(factor_old, left, right, total, rid[:, None] == cid[None, :], d0)
    swept = factor - jnp.dot(both, Q, precision=lax.Precision.HIGH, preferred_element_type=f32)
    owner2 = spacing // rows
    extra = jnp.where(rows1, q1, jnp.where(shard == owner2, q2, 0.0))
    swept = swept.at[:BLOCK].add(extra)
    half_swept = swept.astype(bf16)
    out = []
    for g in gathered:
        piece = g.reshape(-1, cols)
        width = piece.shape[0] // PIVOTS
        part = lax.dot_general(half_swept, piece, (((1,), (1,)), ((), ())), preferred_element_type=f32)
        theirs = lax.dynamic_slice_in_dim(part, (1 - group) * width, width, 1).astype(bf16)
        sent = lax.ppermute(theirs, "group", swap)
        ours = lax.dynamic_slice_in_dim(part, group * width, width, 1)
        out.append((ours + sent.astype(f32)).astype(bf16).reshape(rows, half_count, 1, units))
    update = jnp.concatenate(out, axis=2).reshape(rows, -1)
    return (swept, update)


def solution(mesh):
    sizes = dict(mesh.shape)
    paired = sizes["group"] == PIVOTS == 2 and D // sizes["shard"] >= BLOCK
    paired = paired and sizes["shard"] >= 4 and sizes["shard"] & (sizes["shard"] - 1) == 0
    return jax.shard_map(
        on_device_pairs if paired else on_device,
        mesh=mesh,
        in_specs=(P("shard", None), P("shard", "group"), P(), P("shard", "group")),
        out_specs=(P("shard", "group"), P("shard", "group")),
        check_vma=False,
    )
```

```python
import jax
import jax.numpy as jnp
from jax import lax
from jax.sharding import PartitionSpec as P

D = 8192
BLOCK = 128
PIVOTS = 2


ema_keep = 0.5


def spread(block, axis, holder):
    block = jnp.where(lax.axis_index(axis) == holder, block, jnp.zeros_like(block))
    return lax.psum(block, axis)


def solve_spd(pivot_block, right_side):
    lower_factor = jnp.linalg.cholesky(pivot_block)
    half_solved = lax.linalg.triangular_solve(lower_factor, right_side, left_side=True, lower=True)
    return lax.linalg.triangular_solve(
        lower_factor, half_solved, left_side=True, lower=True, transpose_a=True
    )


def on_device(samples, factor_old, damping, gradients):
    row_count, col_count = factor_old.shape
    shard_index = lax.axis_index("shard")
    group_index = lax.axis_index("group")
    row_first = shard_index * row_count
    col_first = group_index * col_count
    total_tokens = samples.shape[0] * lax.axis_size("shard")
    contract = (((0,), (0,)), ((), ()))
    token_piece = lax.all_gather(samples, "shard", axis=0, tiled=True)
    left_part = lax.dynamic_slice_in_dim(token_piece, row_first, row_count, 1)
    right_part = lax.dynamic_slice_in_dim(token_piece, col_first, col_count, 1)
    covariance = lax.dot_general(
        left_part, right_part, contract, preferred_element_type=jnp.float32
    )
    row_ids = lax.broadcasted_iota(jnp.int32, (row_count, col_count), 0) + row_first
    col_ids = lax.broadcasted_iota(jnp.int32, (row_count, col_count), 1) + col_first
    diagonal = jnp.where(row_ids == col_ids, damping[0], 0.0)
    factor = ema_keep * factor_old + (1.0 - ema_keep) * (covariance / total_tokens) + diagonal
    spacing = D // PIVOTS
    sel_rows = lax.broadcasted_iota(jnp.int32, (BLOCK, col_count), 0)
    sel_cols = lax.broadcasted_iota(jnp.int32, (BLOCK, col_count), 1) + col_first

    def sweep_once(sweep_step, matrix):
        first_index = (sweep_step * spacing).astype(jnp.int32)
        col_owner = first_index // col_count
        row_owner = first_index // row_count
        col_offset = first_index - col_owner * col_count
        row_offset = first_index - row_owner * row_count
        own_columns = lax.dynamic_slice_in_dim(matrix, col_offset, BLOCK, 1)
        column = spread(own_columns, "group", col_owner)
        own_rows = lax.dynamic_slice_in_dim(matrix, row_offset, BLOCK, 0)
        own_pivot = lax.dynamic_slice_in_dim(column, row_offset, BLOCK, 0)
        pivot_strip, pivot_block = (
            spread(own_rows, "shard", row_owner),
            spread(own_pivot, "shard", row_owner),
        )
        selector = jnp.where(sel_cols == sel_rows + first_index, 1.0, 0.0).astype(jnp.float32)
        factor_q = solve_spd(pivot_block, pivot_strip + selector)
        matrix = matrix - jnp.dot(
            column, factor_q, precision=lax.Precision.HIGHEST, preferred_element_type=jnp.float32
        )
        addition = jnp.where(shard_index == row_owner, factor_q, 0.0)
        block_rows = lax.dynamic_slice_in_dim(matrix, row_offset, BLOCK, 0) + addition
        return lax.dynamic_update_slice_in_dim(matrix, block_rows, row_offset, 0)

    swept_factor = lax.fori_loop(0, PIVOTS, sweep_once, factor)
    swept_half = swept_factor.astype(jnp.bfloat16)
    partial_terms = lax.dot_general(
        swept_half,
        lax.all_gather(gradients, "shard", axis=0, tiled=True),
        (((1,), (1,)), ((), ())),
        preferred_element_type=jnp.float32,
    )
    update = lax.psum_scatter(partial_terms, "group", scatter_dimension=1, tiled=True).astype(
        jnp.bfloat16
    )
    return (swept_factor, update)


def damped(old, left, right, total, hit, damping):
    cov = lax.dot_general(left, right, (((0,), (0,)), ((), ())), preferred_element_type=jnp.float32)
    return ema_keep * old + (1.0 - ema_keep) * (cov / total) + jnp.where(hit, damping, 0.0)


def exact(a, b):
    return jnp.dot(a, b, precision=lax.Precision.HIGHEST, preferred_element_type=jnp.float32)


def on_device_pairs(samples, factor_old, damping, gradients):
    rows, cols = factor_old.shape
    shards = lax.axis_size("shard")
    shard = lax.axis_index("shard")
    group = lax.axis_index("group")
    row_first, col_first = shard * rows, group * cols
    total = samples.shape[0] * shards
    wide = PIVOTS * BLOCK
    bf16, f32 = jnp.bfloat16, jnp.float32
    half_count = shards // PIVOTS
    shard_half = shard // half_count
    own = lax.optimization_barrier(factor_old[:, :BLOCK]).T
    high = own.astype(bf16)
    low = (own[:, :BLOCK] - high[:, :BLOCK].astype(f32)).astype(bf16)
    swap = [(0, 1), (1, 0)]

    def ordered(first, mine, other, axis):
        return jnp.concatenate([jnp.where(first, mine, other), jnp.where(first, other, mine)], axis=axis)

    across = [(i, i ^ half_count) for i in range(shards)]
    bits = [1 << k for k in range(half_count.bit_length() - 1)]
    tops = jnp.stack([high[:, :BLOCK], low])
    tops = ordered(group == 0, tops, lax.ppermute(tops, "group", swap), 1)
    ends = [(i, j) for i, j in across if i % half_count == 0]
    tops = ordered(shard_half == 0, tops, lax.ppermute(tops, "shard", ends), 2)
    tokens = jnp.concatenate([samples, lax.ppermute(samples, "shard", across)], axis=0)
    for bit in bits[::-1]:
        tree = [(i, i ^ bit) for i in range(shards) if i % (2 * bit) == 0]
        tops = jnp.where(shard % (2 * bit) == bit, lax.ppermute(tops, "shard", tree), tops)
        other = lax.ppermute(tokens, "shard", [(i, i ^ bit) for i in range(shards)])
        tokens = jnp.concatenate([tokens, other], axis=0)
    tops = tops.astype(f32)
    pair = ordered(group == 0, high, lax.ppermute(high, "group", swap), 0)
    one_way = [(g * shards + i, g * shards + (i ^ half_count))
               for g in range(PIVOTS) for i in range(shards) if i // half_count == g]
    moved = lax.ppermute(pair, ("group", "shard"), one_way)
    held = jnp.where(shard_half == group, pair, moved)
    for bit in bits[1:]:
        other = lax.ppermute(held, "shard", [(i, i ^ bit) for i in range(shards)])
        held = ordered((shard & bit) == 0, held, other, 1)
    other = lax.ppermute(held, "shard", [(i, i ^ 1) for i in range(shards)])
    even, odd = jnp.where(shard % 2 == 0, held, other), jnp.where(shard % 2 == 0, other, held)
    strip = jnp.concatenate([piece[:, i:i + rows] for i in range(0, even.shape[1], rows)
                             for piece in (even, odd)], axis=1).astype(f32)
    units = gradients.shape[0] // 2
    gathered = []
    for half in range(2):
        piece = gradients[half * units:(half + 1) * units]
        gathered.append(lax.all_gather(piece, "shard", axis=0, tiled=False))
    spacing = D // PIVOTS
    ptok = jnp.concatenate([tokens[:, p * spacing:p * spacing + BLOCK] for p in range(PIVOTS)], axis=1)
    pidx = jnp.concatenate([jnp.arange(BLOCK) + p * spacing for p in range(PIVOTS)])
    left = lax.dynamic_slice_in_dim(tokens, row_first, rows, 1)
    right = lax.dynamic_slice_in_dim(tokens, col_first, cols, 1)
    rid = jnp.arange(rows) + row_first
    cid = jnp.arange(cols) + col_first
    d0 = damping[0]
    col_own = pair.T.astype(f32)
    C = damped(col_own, left, ptok, total, rid[:, None] == pidx[None, :], d0)
    R = damped(strip, ptok, right, total, pidx[:, None] == cid[None, :], d0)
    A = damped(tops[0] + tops[1], ptok, ptok, total, pidx[:, None] == pidx[None, :], d0)
    E = jnp.where(pidx[:, None] == cid[None, :], 1.0, 0.0).astype(f32)
    ones = jnp.eye(BLOCK, dtype=f32)
    a, b = slice(0, BLOCK), slice(BLOCK, wide)
    inv1 = solve_spd(A[a, a], ones)
    q1 = exact(inv1, R[a] + E[a])
    cross = exact(inv1, A[a, b])
    A22 = A[b, b] - exact(A[b, a], cross)
    inv2 = solve_spd(A22, ones)
    q2 = exact(inv2, R[b] - exact(A[b, a], q1) + E[b])
    rows1 = shard == 0
    C2 = C[:, b] - exact(C[:, a], cross)
    add = jnp.where(rows1, cross, 0.0)
    C2 = C2.at[:BLOCK].add(add)
    Q = jnp.concatenate([q1, q2], axis=0)
    both = jnp.concatenate([C[:, a], C2], axis=1)
    factor = damped(factor_old, left, right, total, rid[:, None] == cid[None, :], d0)
    swept = factor - jnp.dot(both, Q, precision=lax.Precision.HIGH, preferred_element_type=f32)
    owner2 = spacing // rows
    extra = jnp.where(rows1, q1, jnp.where(shard == owner2, q2, 0.0))
    swept = swept.at[:BLOCK].add(extra)
    half_swept = swept.astype(bf16)
    out = []
    for g in gathered:
        piece = g.reshape(-1, cols)
        width = piece.shape[0] // PIVOTS
        part = lax.dot_general(half_swept, piece, (((1,), (1,)), ((), ())), preferred_element_type=f32)
        theirs = lax.dynamic_slice_in_dim(part, (1 - group) * width, width, 1).astype(bf16)
        sent = lax.ppermute(theirs, "group", swap)
        ours = lax.dynamic_slice_in_dim(part, group * width, width, 1)
        out.append((ours + sent.astype(f32)).astype(bf16).reshape(rows, half_count, 1, units))
    update = jnp.concatenate(out, axis=2).reshape(rows, -1)
    return (swept, update)


def solution(mesh):
    sizes = dict(mesh.shape)
    paired = sizes["group"] == PIVOTS == 2 and D // sizes["shard"] >= BLOCK
    paired = paired and sizes["shard"] >= 4 and sizes["shard"] & (sizes["shard"] - 1) == 0
    return jax.shard_map(
        on_device_pairs if paired else on_device,
        mesh=mesh,
        in_specs=(P("shard", None), P("shard", "group"), P(), P("shard", "group")),
        out_specs=(P("shard", "group"), P("shard", "group")),
        check_vma=False,
    )
```

```python
import jax
import jax.numpy as jnp
from jax import lax
from jax.sharding import PartitionSpec as P

D = 8192
BLOCK = 128
PIVOTS = 2


ema_keep = 0.5


def spread(block, axis, holder):
    block = jnp.where(lax.axis_index(axis) == holder, block, jnp.zeros_like(block))
    return lax.psum(block, axis)


def solve_spd(pivot_block, right_side):
    lower_factor = jnp.linalg.cholesky(pivot_block)
    half_solved = lax.linalg.triangular_solve(lower_factor, right_side, left_side=True, lower=True)
    return lax.linalg.triangular_solve(
        lower_factor, half_solved, left_side=True, lower=True, transpose_a=True
    )


def on_device(samples, factor_old, damping, gradients):
    row_count, col_count = factor_old.shape
    shard_index = lax.axis_index("shard")
    group_index = lax.axis_index("group")
    row_first = shard_index * row_count
    col_first = group_index * col_count
    total_tokens = samples.shape[0] * lax.axis_size("shard")
    contract = (((0,), (0,)), ((), ()))
    token_piece = lax.all_gather(samples, "shard", axis=0, tiled=True)
    left_part = lax.dynamic_slice_in_dim(token_piece, row_first, row_count, 1)
    right_part = lax.dynamic_slice_in_dim(token_piece, col_first, col_count, 1)
    covariance = lax.dot_general(
        left_part, right_part, contract, preferred_element_type=jnp.float32
    )
    row_ids = lax.broadcasted_iota(jnp.int32, (row_count, col_count), 0) + row_first
    col_ids = lax.broadcasted_iota(jnp.int32, (row_count, col_count), 1) + col_first
    diagonal = jnp.where(row_ids == col_ids, damping[0], 0.0)
    factor = ema_keep * factor_old + (1.0 - ema_keep) * (covariance / total_tokens) + diagonal
    spacing = D // PIVOTS
    sel_rows = lax.broadcasted_iota(jnp.int32, (BLOCK, col_count), 0)
    sel_cols = lax.broadcasted_iota(jnp.int32, (BLOCK, col_count), 1) + col_first

    def sweep_once(sweep_step, matrix):
        first_index = (sweep_step * spacing).astype(jnp.int32)
        col_owner = first_index // col_count
        row_owner = first_index // row_count
        col_offset = first_index - col_owner * col_count
        row_offset = first_index - row_owner * row_count
        own_columns = lax.dynamic_slice_in_dim(matrix, col_offset, BLOCK, 1)
        column = spread(own_columns, "group", col_owner)
        own_rows = lax.dynamic_slice_in_dim(matrix, row_offset, BLOCK, 0)
        own_pivot = lax.dynamic_slice_in_dim(column, row_offset, BLOCK, 0)
        pivot_strip, pivot_block = (
            spread(own_rows, "shard", row_owner),
            spread(own_pivot, "shard", row_owner),
        )
        selector = jnp.where(sel_cols == sel_rows + first_index, 1.0, 0.0).astype(jnp.float32)
        factor_q = solve_spd(pivot_block, pivot_strip + selector)
        matrix = matrix - jnp.dot(
            column, factor_q, precision=lax.Precision.HIGHEST, preferred_element_type=jnp.float32
        )
        addition = jnp.where(shard_index == row_owner, factor_q, 0.0)
        block_rows = lax.dynamic_slice_in_dim(matrix, row_offset, BLOCK, 0) + addition
        return lax.dynamic_update_slice_in_dim(matrix, block_rows, row_offset, 0)

    swept_factor = lax.fori_loop(0, PIVOTS, sweep_once, factor)
    swept_half = swept_factor.astype(jnp.bfloat16)
    partial_terms = lax.dot_general(
        swept_half,
        lax.all_gather(gradients, "shard", axis=0, tiled=True),
        (((1,), (1,)), ((), ())),
        preferred_element_type=jnp.float32,
    )
    update = lax.psum_scatter(partial_terms, "group", scatter_dimension=1, tiled=True).astype(
        jnp.bfloat16
    )
    return (swept_factor, update)


def damped(old, left, right, total, hit, damping):
    cov = lax.dot_general(left, right, (((0,), (0,)), ((), ())), preferred_element_type=jnp.float32)
    return ema_keep * old + (1.0 - ema_keep) * (cov / total) + jnp.where(hit, damping, 0.0)


def exact(a, b):
    return jnp.dot(a, b, precision=lax.Precision.HIGHEST, preferred_element_type=jnp.float32)


def on_device_pairs(samples, factor_old, damping, gradients):
    rows, cols = factor_old.shape
    shards = lax.axis_size("shard")
    shard = lax.axis_index("shard")
    group = lax.axis_index("group")
    row_first, col_first = shard * rows, group * cols
    total = samples.shape[0] * shards
    wide = PIVOTS * BLOCK
    bf16, f32 = jnp.bfloat16, jnp.float32
    half_count = shards // PIVOTS
    shard_half = shard // half_count
    own = lax.optimization_barrier(factor_old[:, :BLOCK]).T
    high = own.astype(bf16)
    low = (own[:, :BLOCK] - high[:, :BLOCK].astype(f32)).astype(bf16)
    swap = [(0, 1), (1, 0)]

    def ordered(first, mine, other, axis):
        return jnp.concatenate([jnp.where(first, mine, other), jnp.where(first, other, mine)], axis=axis)

    across = [(i, i ^ half_count) for i in range(shards)]
    bits = [1 << k for k in range(half_count.bit_length() - 1)]
    tops = jnp.stack([high[:, :BLOCK], low])
    tops = ordered(group == 0, tops, lax.ppermute(tops, "group", swap), 1)
    ends = [(i, j) for i, j in across if i % half_count == 0]
    tops = ordered(shard_half == 0, tops, lax.ppermute(tops, "shard", ends), 2)
    tokens = jnp.concatenate([samples, lax.ppermute(samples, "shard", across)], axis=0)
    for bit in bits[::-1]:
        tree = [(i, i ^ bit) for i in range(shards) if i % (2 * bit) == 0]
        tops = jnp.where(shard % (2 * bit) == bit, lax.ppermute(tops, "shard", tree), tops)
        other = lax.ppermute(tokens, "shard", [(i, i ^ bit) for i in range(shards)])
        tokens = jnp.concatenate([tokens, other], axis=0)
    tops = tops.astype(f32)
    pair = ordered(group == 0, high, lax.ppermute(high, "group", swap), 0)
    one_way = [(g * shards + i, g * shards + (i ^ half_count))
               for g in range(PIVOTS) for i in range(shards) if i // half_count == g]
    moved = lax.ppermute(pair, ("group", "shard"), one_way)
    held = jnp.where(shard_half == group, pair, moved)
    for bit in bits[1:]:
        other = lax.ppermute(held, "shard", [(i, i ^ bit) for i in range(shards)])
        held = ordered((shard & bit) == 0, held, other, 1)
    other = lax.ppermute(held, "shard", [(i, i ^ 1) for i in range(shards)])
    even, odd = jnp.where(shard % 2 == 0, held, other), jnp.where(shard % 2 == 0, other, held)
    strip = jnp.concatenate([piece[:, i:i + rows] for i in range(0, even.shape[1], rows)
                             for piece in (even, odd)], axis=1).astype(f32)
    most = gradients.shape[0] * 3 // 4
    gathered = [lax.all_gather(piece, "shard", axis=0, tiled=False)
                for piece in (gradients[:most], gradients[most:])]
    spacing = D // PIVOTS
    ptok = jnp.concatenate([tokens[:, p * spacing:p * spacing + BLOCK] for p in range(PIVOTS)], axis=1)
    pidx = jnp.concatenate([jnp.arange(BLOCK) + p * spacing for p in range(PIVOTS)])
    left = lax.dynamic_slice_in_dim(tokens, row_first, rows, 1)
    right = lax.dynamic_slice_in_dim(tokens, col_first, cols, 1)
    rid = jnp.arange(rows) + row_first
    cid = jnp.arange(cols) + col_first
    d0 = damping[0]
    col_own = pair.T.astype(f32)
    C = damped(col_own, left, ptok, total, rid[:, None] == pidx[None, :], d0)
    R = damped(strip, ptok, right, total, pidx[:, None] == cid[None, :], d0)
    A = damped(tops[0] + tops[1], ptok, ptok, total, pidx[:, None] == pidx[None, :], d0)
    E = jnp.where(pidx[:, None] == cid[None, :], 1.0, 0.0).astype(f32)
    ones = jnp.eye(BLOCK, dtype=f32)
    a, b = slice(0, BLOCK), slice(BLOCK, wide)
    inv1 = solve_spd(A[a, a], ones)
    q1 = exact(inv1, R[a] + E[a])
    cross = exact(inv1, A[a, b])
    A22 = A[b, b] - exact(A[b, a], cross)
    inv2 = solve_spd(A22, ones)
    q2 = exact(inv2, R[b] - exact(A[b, a], q1) + E[b])
    rows1 = shard == 0
    C2 = C[:, b] - exact(C[:, a], cross)
    add = jnp.where(rows1, cross, 0.0)
    C2 = C2.at[:BLOCK].add(add)
    Q = jnp.concatenate([q1, q2], axis=0)
    both = jnp.concatenate([C[:, a], C2], axis=1)
    factor = damped(factor_old, left, right, total, rid[:, None] == cid[None, :], d0)
    swept = factor - jnp.dot(both, Q, precision=lax.Precision.HIGH, preferred_element_type=f32)
    owner2 = spacing // rows
    extra = jnp.where(rows1, q1, jnp.where(shard == owner2, q2, 0.0))
    swept = swept.at[:BLOCK].add(extra)
    half_swept = swept.astype(bf16)
    out = []
    for g in gathered:
        piece = g.reshape(-1, cols)
        width = piece.shape[0] // PIVOTS
        part = lax.dot_general(half_swept, piece, (((1,), (1,)), ((), ())), preferred_element_type=f32)
        theirs = lax.dynamic_slice_in_dim(part, (1 - group) * width, width, 1).astype(bf16)
        sent = lax.ppermute(theirs, "group", swap)
        ours = lax.dynamic_slice_in_dim(part, group * width, width, 1)
        out.append((ours + sent.astype(f32)).astype(bf16).reshape(rows, half_count, -1))
    update = jnp.concatenate(out, axis=2).reshape(rows, -1)
    return (swept, update)


def solution(mesh):
    sizes = dict(mesh.shape)
    paired = sizes["group"] == PIVOTS == 2 and D // sizes["shard"] >= BLOCK
    paired = paired and sizes["shard"] >= 4 and sizes["shard"] & (sizes["shard"] - 1) == 0
    return jax.shard_map(
        on_device_pairs if paired else on_device,
        mesh=mesh,
        in_specs=(P("shard", None), P("shard", "group"), P(), P("shard", "group")),
        out_specs=(P("shard", "group"), P("shard", "group")),
        check_vma=False,
    )
```
